1024 devices in a mesh: node: 64 (over x, z), local: 16 (over y, core).
Axes of the slice: x: 8, y: 8, z: 8, core: 2. Of those that a mesh axis runs over, the one named last changes fastest.
Arguments:
- grad_out: bfloat16 [8192, 6144], P('node', 'local'), may hold values from -6 to 6
- gate_prob: float32 [8192, 8], P('node'), may hold values from 0.05 to 0.5
- routes: int32 [8192, 8], P('node'), may hold values from 0 to 63, all different within a row; in each aligned block of 128 rows (0 to 127, 128 to 255, ...) at most 16 rows name the same one
- paired: int32 [32], replicated, may hold values from 0 to 1, as said below
- saved_pre: bfloat16 [64, 64, 16, 2, 1024], P('node'), may hold values from -6 to 6
- w_gate: bfloat16 [64, 6144, 1024], P('node', 'local'), may hold values from -0.078125 to 0.078125
- w_up: bfloat16 [64, 6144, 1024], P('node', 'local'), may hold values from -0.078125 to 0.078125
- w_down: bfloat16 [64, 1024, 6144], P('node', None, 'local'), may hold values from -0.1875 to 0.1875
Outputs:
- grad_in: bfloat16 [8192, 6144], P('node', 'local')
- grad_down: bfloat16 [64, 1024, 6144], P('node', None, 'local')
The draws below stay inside these ranges and needn't reach their ends.
Inputs may be any that keep to these rules, and one draw needn't show every extreme that they name: `routes`: each token names 8 different slots. Within the 128 tokens of one block (one index of node), no slot is named by more than 16 tokens, a bound that some block reaches. Exactly half of the pairs are paired, which ones drawn from the seed.
All inputs are finite; a program needn't handle non-finite values.
Results may differ from the reference program's by a relative error of at most 0.023.
Values may be sent and summed in bfloat16 or wider, within the bound.
A program may use at most 64 MiB of HBM per device.

```python
import math
import jax
import jax.numpy as jnp
import numpy as np
from jax import lax

D = 6144
EXPERT_HIDDEN = 1024
TOP = 8
TOK_NODE = 128
C = 16
TOKENS = 8192
N_NODE = 64
N_LOCAL = 16


def draw_paired(key, part):
    order = jax.random.permutation(key, N_NODE // 2)
    return (order % 2).astype(jnp.int32)


def levels(own_key, extent, split, least, high):
    level, own = 1.0, jax.random.fold_in(own_key, 6)
    for dim, parts in split:
        heights = jnp.exp(jax.random.uniform(jax.random.fold_in(own, dim), (parts,), jnp.float32, least / len(split), high / len(split)))
        level = level * jnp.repeat(heights, extent[dim] // parts).reshape([-1 if axis == dim else 1 for axis in range(len(extent))])
    return level


def assign_block(own_key, own, number, rows, amount, top, reach, skew):
    ranking = jax.random.permutation(own_key, amount)
    packed, common = shares(amount, rows * top, reach, skew, True), shares(amount, rows * top, reach, skew, False)
    places = jnp.arange(amount)

    def named(tallies, rotation):
        used = int((tallies > 0).sum())
        fixed = max(1, used // 4)
        shifted = fixed + (places - fixed + rotation * (used - fixed)) % max(1, amount - fixed)
        return jnp.zeros((amount,), jnp.int32).at[ranking[jnp.where(places < fixed, places, shifted)]].set(jnp.asarray(tallies, jnp.int32))

    tallies = jnp.where(number % 4 == 0, named(packed, number // 4), named(common, number - number // 4 - 1))
    mixed = jax.random.permutation(jax.random.fold_in(own, 3), amount)
    source_of, taker = mixed[0:amount // 2 * 2:2], mixed[1:amount // 2 * 2:2]
    margin = jnp.minimum(tallies[source_of] - 1, reach - tallies[taker]) // 2
    margin = jnp.where((source_of == ranking[0]) | (taker == ranking[0]) | (tallies[taker] == 0), 0, jnp.maximum(margin, 0))
    shifted = jax.random.randint(jax.random.fold_in(own, 4), (amount // 2,), 0, 1 << 20) % (margin + 1)
    tallies = tallies.at[source_of].add(-shifted).at[taker].add(shifted)
    members = jnp.searchsorted(jnp.cumsum(tallies), jnp.arange(rows * top), side="right").astype(jnp.int32)
    table = members.reshape(top, rows).T
    table = table[jax.random.permutation(jax.random.fold_in(own, 1), rows)]
    rotation = jax.random.randint(jax.random.fold_in(own, 2), (rows, 1), 0, top)
    return jnp.take_along_axis(table, (jnp.arange(top)[None, :] + rotation) % top, axis=1)


def shares(number_of, total, bound, skew, full):
    weights = [(1 << 20) // math.isqrt(grade ** skew) + 1 for grade in range(1, number_of + 1)]
    largest = bound if full else min(bound, max(-(-total // number_of), total * weights[0] // sum(weights)))
    least = 1 if total - largest >= number_of - 1 else 0
    given, rest = [largest] + [least] * (number_of - 1), total - largest - least * (number_of - 1)
    while rest > 0:
        candidates = [i for i in range(1, number_of) if given[i] < largest] or [i for i in range(1, number_of) if given[i] < bound]
        mass, left = sum([weights[i] for i in candidates]), rest
        for i in candidates:
            extra = min(bound - given[i], max(1, left * weights[i] // mass), rest)
            given[i] = given[i] + extra
            rest = rest - extra
    return np.array(given)


def centred(rng, shape, width, bound, pieces=(), kind=jnp.bfloat16):
    result = jax.random.normal(rng, shape, jnp.float32) * width
    if len(pieces) > 0:
        result = levels(rng, shape, pieces, -0.22, 0.18) * result
    return jnp.clip(result, min=-bound, max=bound).astype(kind)


def setup_inputs(seed: int = 0) -> dict:
    key_of = jax.random.split(jax.random.key(seed), 9)
    grad_out = centred(key_of[0], (TOKENS, D), 1.0, 6.0, ((0, 64), (1, 16)))
    gate_prob = jnp.clip(jnp.exp(math.log(0.5) - 2.3025851 * jax.random.uniform(key_of[1], (TOKENS, TOP), jnp.float32) ** levels(key_of[1], (TOKENS, TOP), ((0, 64),), -0.2, 0.2)), 0.05, 0.5)
    routes_keys = jax.random.split(jax.random.fold_in(key_of[2], 1), TOKENS // TOK_NODE)
    routes_turns = jax.random.permutation(jax.random.fold_in(key_of[2], 3), TOKENS // TOK_NODE)
    routes = jax.vmap(lambda own, number: assign_block(jax.random.fold_in(key_of[2], 2), own, number, TOK_NODE, N_NODE, TOP, C, 2))(routes_keys, routes_turns).reshape((TOKENS, TOP))
    paired = draw_paired(jax.random.fold_in(key_of[8], 71), 0)
    saved_pre = centred(key_of[4], (N_NODE, N_NODE, C, 2, EXPERT_HIDDEN), 1.0, 6.0, ((0, 64),))
    w_gate = centred(key_of[5], (N_NODE, D, EXPERT_HIDDEN), D ** -0.5, 0.078125, ((0, 64), (1, 16)))
    w_up = centred(key_of[6], (N_NODE, D, EXPERT_HIDDEN), D ** -0.5, 0.078125, ((0, 64), (1, 16)))
    w_down = centred(key_of[7], (N_NODE, EXPERT_HIDDEN, D), EXPERT_HIDDEN ** -0.5, 0.1875, ((0, 64), (2, 16)))
    return dict(grad_out=grad_out, gate_prob=gate_prob, routes=routes, paired=paired, saved_pre=saved_pre, w_gate=w_gate, w_up=w_up, w_down=w_down)


def swiglu_back(dhid, pre):
    gval = pre[:, 0, :].astype(jnp.float32)
    uval = pre[:, 1, :].astype(jnp.float32)
    sigm = jax.nn.sigmoid(gval)
    silu_val = gval * sigm
    dgate = (dhid * uval * sigm * (1.0 + gval * (1.0 - sigm))).astype(jnp.bfloat16)
    dup = (dhid * silu_val).astype(jnp.bfloat16)
    act = (silu_val * uval).astype(jnp.bfloat16)
    return dgate, dup, act


def reference(grad_out, gate_prob, routes, paired, saved_pre, w_gate, w_up, w_down):
    blocks = routes.reshape(N_NODE, TOK_NODE * TOP)
    experts_row = jnp.arange(N_NODE, dtype=jnp.int32)
    onehot = (blocks[:, :, None] == experts_row[None, None, :]).astype(jnp.int32)
    before = jnp.cumsum(onehot, axis=1) - onehot
    row_rank = jnp.sum(before * onehot, axis=2).astype(jnp.int32)
    source = jnp.broadcast_to(jnp.arange(N_NODE, dtype=jnp.int32)[:, None], blocks.shape)
    flat_index = jnp.arange(TOKENS * TOP, dtype=jnp.int32).reshape(N_NODE, TOK_NODE * TOP)
    table = jnp.full((N_NODE, N_NODE, C), -1, jnp.int32)
    table = table.at[blocks.reshape(-1), source.reshape(-1), row_rank.reshape(-1)].set(flat_index.reshape(-1))
    rows_per_slot = N_NODE * C
    part_slice = D // N_LOCAL

    def one_slot(expert):
        index_row = table[expert].reshape(rows_per_slot)
        valid = index_row >= 0
        safe = jnp.where(valid, index_row, 0)
        token_id = safe // TOP
        which = safe - token_id * TOP
        scale = gate_prob[token_id, which] * valid.astype(jnp.float32)
        token_rows = (grad_out[token_id].astype(jnp.float32) * scale[:, None]).astype(jnp.bfloat16)
        down_matrix = w_down[expert]
        part_count = jnp.einsum("ugp,tgp->gut", token_rows.reshape(rows_per_slot, N_LOCAL, part_slice).astype(jnp.float32), down_matrix.reshape(EXPERT_HIDDEN, N_LOCAL, part_slice).astype(jnp.float32))
        part_count = part_count.astype(jnp.bfloat16)
        dhid = jnp.sum(part_count.astype(jnp.float32), axis=0)
        pre = saved_pre[expert].reshape(rows_per_slot, 2, EXPERT_HIDDEN)
        dgate, dup, act = swiglu_back(dhid, pre)
        back = jnp.dot(dgate, w_gate[expert].T, preferred_element_type=jnp.float32) + jnp.dot(dup, w_up[expert].T, preferred_element_type=jnp.float32)
        back = back.astype(jnp.bfloat16)
        own = jnp.dot(act.T, token_rows, preferred_element_type=jnp.float32).astype(jnp.bfloat16)
        return back, own

    backs, owns = lax.map(one_slot, jnp.arange(N_NODE, dtype=jnp.int32))
    targets = table.reshape(-1)
    targets = jnp.where(targets >= 0, targets, TOKENS * TOP)
    spread_rows = jnp.zeros((TOKENS * TOP, D), jnp.bfloat16).at[targets].set(backs.reshape(N_NODE * rows_per_slot, D), mode="drop")
    grad_in = jnp.sum(spread_rows.reshape(TOKENS, TOP, D).astype(jnp.float32), axis=1).astype(jnp.bfloat16)
    partner = jnp.roll(owns, N_NODE // 2, axis=0)
    flags = jnp.concatenate([paired, paired]).astype(jnp.float32)
    own_f = lax.optimization_barrier(owns).astype(jnp.float32)
    grad_down = (own_f + flags[:, None, None] * partner.astype(jnp.float32)).astype(jnp.bfloat16)
    return grad_in, grad_down
```

```python
import functools

import jax
import jax.numpy as jnp
from jax import lax
from jax.experimental import pallas as pl
from jax.experimental.pallas import tpu as pltpu
from jax.sharding import PartitionSpec as P

MESH = pl.DeviceIdType.MESH
DEPTH = 8
F32 = jnp.float32
BF16 = jnp.bfloat16
NT = (((1,), (1,)), ((), ()))
PIECES = 2


def remote(src, dst, send, recv, **where):
    return pltpu.make_async_remote_copy(
        src_ref=src, dst_ref=dst, send_sem=send, recv_sem=recv, device_id=where, device_id_type=MESH
    )


def local_copy(src, dst, sem):
    return pltpu.make_async_copy(src, dst, sem)


def kernel(
    depth,
    grad_out, gate, routes, paired, pre_hbm, wg_hbm, wu_hbm, wd_hbm,
    gin, gdown,
    code, gates, onehot, rows_out, rows_in, pre, wg, wu, wd, fgate, fup, act, act_t,
    part, mate, long_out, long_in, short_out, short_in, dhid, back, homing, own, other,
    pre_sem, w_sem, rows_send, rows_recv, mate_send, mate_recv,
    long_send, long_recv, short_send, short_recv, own_send, own_recv,
    up_send, up_recv, down_send, down_recv, core_send, core_recv, home_send, home_recv,
):
    nodes, cap, feat = rows_out.shape
    slabs = part.shape[0]
    hidden = part.shape[3]
    share = part.shape[2]
    block = 2 * share
    group = nodes // slabs
    wide = nodes // depth
    tops, toks = routes.shape
    far, near = slabs // 2, slabs - 1 - slabs // 2
    size = share // PIECES

    me = lax.axis_index("node")
    at = lax.axis_index("local")
    my_x, my_z = me // depth, me % depth
    my_y, core = at // 2, at % 2
    sign = 1 - 2 * core
    mate_at = my_y * 2 + 1 - core

    def slab_of(step):
        return lax.rem(my_y + step + slabs, slabs)

    ahead = slab_of(sign) * 2 + core
    behind = slab_of(-sign) * 2 + core

    def offset_of(place):
        q, dz = place // depth, place % depth
        return lax.rem(q - dz + wide * depth, wide), dz

    def node_ahead(dx, dz):
        return lax.rem(my_x + dx, wide) * depth + lax.rem(my_z + dz, depth)

    def node_back(dx, dz):
        return lax.rem(my_x - dx + wide, wide) * depth + lax.rem(my_z - dz + depth, depth)

    def turn(i):
        k = far - (i + 1) // 2
        return lax.rem(my_y + jnp.where(i % 2 == 0, -k, k) + slabs, slabs)

    barrier = pltpu.get_barrier_semaphore()

    def greet(k, carry):
        pl.semaphore_signal(barrier, inc=1, device_id={"node": lax.rem(me + k, nodes)}, device_id_type=MESH)
        return carry

    lax.fori_loop(1, nodes, greet, 0)
    for other_at in (mate_at, ahead, behind):
        pl.semaphore_signal(barrier, inc=1, device_id={"local": other_at}, device_id_type=MESH)

    loads = [local_copy(a.at[0], b, w_sem.at[i]) for i, (a, b) in enumerate(((wd_hbm, wd), (wg_hbm, wg), (wu_hbm, wu)))]

    def load_pre(place, carry):
        dx, dz = offset_of(place)
        local_copy(pre_hbm.at[0, node_ahead(dx, dz)], pre.at[place], pre_sem.at[place // group]).start()
        return carry

    lax.fori_loop(0, nodes, load_pre, 0)
    for load in loads:
        load.start()

    slot_id = lax.broadcasted_iota(jnp.int32, (nodes, toks), 0)
    named = jnp.zeros((nodes, toks), F32)
    gate_of = jnp.zeros((nodes, toks), F32)
    for k in range(tops):
        hit = routes[k : k + 1, :] == slot_id
        named = jnp.where(hit, 1.0, named)
        gate_of = jnp.where(hit, gate[k : k + 1, :], gate_of)
    earlier = lax.broadcasted_iota(jnp.int32, (toks, toks), 0) < lax.broadcasted_iota(jnp.int32, (toks, toks), 1)
    rank = jnp.dot(named.astype(BF16), jnp.where(earlier, 1.0, 0.0).astype(BF16), preferred_element_type=F32)
    code[...] = jnp.where(named > 0.0, rank, -1.0)
    gates[...] = gate_of
    some = min(8, nodes)

    def fill(i, carry):
        slots = pl.ds(pl.multiple_of(i * some, some), some)
        want = lax.broadcasted_iota(jnp.int32, (some, cap, toks), 1).astype(F32)
        hit = code[slots, :][:, None, :] == want
        scale = jnp.sum(jnp.where(hit, gates[slots, :][:, None, :], 0.0), axis=2, keepdims=True)
        picks = jnp.where(hit, 1.0, 0.0).reshape(some * cap, toks).astype(BF16)
        onehot[pl.ds(pl.multiple_of(i * some * cap, some * cap), some * cap), :] = picks
        values = jnp.dot(picks, grad_out[...], preferred_element_type=F32)
        values = values.reshape(some, cap, feat) * scale
        rows_out[slots] = values.astype(BF16)
        return carry

    lax.fori_loop(0, nodes // some, fill, 0)

    pl.semaphore_wait(barrier, nodes - 1 + 3)

    def send_rows(n, carry):
        i, dz = n // depth, n % depth
        q = turn(i)
        dx = lax.rem(q - dz + wide * depth, wide)
        target = node_back(dx, dz)
        place = q * depth + dz

        @pl.when(target != me)
        def _():
            remote(rows_out.at[target], rows_in.at[place], rows_send, rows_recv.at[q], node=target).start()

        @pl.when(target == me)
        def _():
            local_copy(rows_out.at[target], rows_in.at[place], rows_recv.at[q]).start()

        return carry

    lax.fori_loop(0, nodes, send_rows, 0)

    def factors(q, carry):
        blocks = pl.ds(pl.multiple_of(q * group, group), group)
        local_copy(pre.at[blocks], pre.at[blocks], pre_sem.at[q]).wait()

        def one(i, carry):
            place = q * group + i
            both = pre[place].astype(F32)
            gval, uval = both[:, 0, :], both[:, 1, :]
            sigm = jax.nn.sigmoid(gval)
            silu = gval * sigm
            these = pl.ds(pl.multiple_of(place * cap, cap), cap)
            fgate[these, :] = uval * sigm * (1.0 + gval * (1.0 - sigm))
            fup[these, :] = silu
            act[pl.ds(pl.multiple_of(i * cap, cap), cap), :] = silu * uval
            return carry

        lax.fori_loop(0, group, one, 0)
        act_t[q] = act[...].T.astype(BF16)
        return carry

    lax.fori_loop(0, slabs, factors, 0)
    loads[0].wait()

    def product(i, carry):
        q = turn(i)
        blocks = pl.ds(pl.multiple_of(q * group, group), group)
        local_copy(rows_in.at[blocks], rows_in.at[blocks], rows_recv.at[q]).wait()
        value = lax.dot_general(rows_in[blocks].reshape(block, feat), wd[...], NT, preferred_element_type=F32)
        part[q] = value.astype(BF16).reshape(2, share, hidden)
        remote(part.at[q, 1 - core], mate.at[q], mate_send.at[q], mate_recv.at[q], local=mate_at).start()
        return carry

    def piece(p):
        return pl.ds(p * size, size)

    def mine(q, p):
        return part[q, core, piece(p), :].astype(F32) + mate[q, piece(p), :].astype(F32)

    def wait_mate(q):
        remote(part.at[q, 1 - core], mate.at[q], mate_send.at[q], mate_recv.at[q], local=mate_at).wait_recv()

    def along(kind, j, p):
        if kind == "long":
            return remote(
                long_out.at[j, piece(p)], long_in.at[j, piece(p)], long_send.at[j, p], long_recv.at[j, p], local=ahead
            )
        return remote(
            short_out.at[j, piece(p)], short_in.at[j, piece(p)], short_send.at[j, p], short_recv.at[j, p], local=behind
        )

    waited = set()

    def reduce_step(j):
        chains = [("long", far - j)] + ([("short", -(near - j))] if j < near else [])
        for _, step in chains:
            if step not in waited:
                wait_mate(slab_of(step * sign))
                waited.add(step)
        for p in range(PIECES):
            for kind, step in chains:
                total = mine(slab_of(step * sign), p)
                if j > 0:
                    along(kind, j - 1, p).wait_recv()
                    total = total + (long_in if kind == "long" else short_in)[j - 1, piece(p), :].astype(F32)
                (long_out if kind == "long" else short_out)[j, piece(p), :] = total.astype(BF16)
                along(kind, j, p).start()

    done = 0
    for j in range(far):
        need = min(slabs, 3 + 2 * j) if near > 0 else slabs
        lax.fori_loop(done, need, product, 0)
        done = need
        reduce_step(j)
    if done < slabs:
        lax.fori_loop(done, slabs, product, 0)

    wide_own = own.shape[1]

    def own_copy(i):
        return remote(
            own.at[i], other.at[i], own_send.at[i], own_recv.at[i], node=lax.rem(me + nodes // 2, nodes)
        )

    def own_piece(i, carry):
        these = pl.ds(pl.multiple_of(i * wide_own, wide_own), wide_own)
        value = jnp.zeros((wide_own, feat), F32)
        for q in range(slabs):
            value = value + jnp.dot(
                act_t[q, these, :], rows_in[q * group : (q + 1) * group].reshape(block, feat), preferred_element_type=F32
            )
        own[i] = value.astype(BF16)
        own_copy(i).start()
        return carry

    lax.fori_loop(0, own.shape[0], own_piece, 0)

    def hop(kind, k, p):
        q = slab_of(-k * sign if kind == "long" else k * sign)
        held = dhid.at[q, core, piece(p)]
        if kind == "long":
            return remote(held, held, up_send.at[k, p], up_recv.at[k, p], local=ahead)
        return remote(held, held, down_send.at[k, p], down_recv.at[k, p], local=behind)

    def cross(step, p):
        q = slab_of(step)
        held = dhid.at[q, core, piece(p)]
        return remote(held, held, core_send.at[q, p], core_recv.at[q, p], local=mate_at)

    wait_mate(my_y)
    for p in range(PIECES):
        total = mine(my_y, p)
        along("long", far - 1, p).wait_recv()
        total = total + long_in[far - 1, piece(p), :].astype(F32)
        if near > 0:
            along("short", near - 1, p).wait_recv()
            total = total + short_in[near - 1, piece(p), :].astype(F32)
        dhid[my_y, core, piece(p), :] = total.astype(BF16)
        hop("long", 0, p).start()
        if near > 0:
            hop("short", 0, p).start()
        cross(0, p).start()

    loads[1].wait()
    loads[2].wait()

    def send_back(n, q):
        place = q * depth + lax.rem(n + my_z, depth)
        dx, dz = offset_of(place)
        target = node_ahead(dx, dz)

        @pl.when(target != me)
        def _():
            remote(back.at[place], homing.at[me], home_send, home_recv.at[me // group], node=target).start()

        @pl.when(target == me)
        def _():
            local_copy(back.at[place], homing.at[me], home_recv.at[me // group]).start()

        return q

    def rows_back(q):
        for p in range(PIECES):
            held = dhid.at[q, 1 - core, piece(p)]
            remote(held, held, core_send.at[q, p], core_recv.at[q, p], local=mate_at).wait_recv()
        these = pl.ds(pl.multiple_of(q * block, block), block)
        value = dhid[q].reshape(block, hidden).astype(F32)
        dgate = (value * fgate[these, :]).astype(BF16)
        dup = (value * fup[these, :]).astype(BF16)
        result = lax.dot_general(dgate, wg[...], NT, preferred_element_type=F32)
        result = result + lax.dot_general(dup, wu[...], NT, preferred_element_type=F32)
        back[pl.ds(pl.multiple_of(q * group, group), group)] = result.astype(BF16).reshape(group, cap, feat)
        lax.fori_loop(0, group, send_back, q)

    def rows_back_pair(k, count):
        def body(i, carry):
            rows_back(slab_of(jnp.where(i == 0, -k, k)))
            return carry

        lax.fori_loop(0, count, body, 0)

    for k in range(1, far + 1):
        for p in range(PIECES):
            hop("long", k - 1, p).wait_recv()
            if k < far:
                hop("long", k, p).start()
            cross(-k * sign, p).start()
            if k <= near:
                hop("short", k - 1, p).wait_recv()
                if k < near:
                    hop("short", k, p).start()
                cross(k * sign, p).start()
        rows_back_pair(k - 1, 1 if k == 1 else 2)
    rows_back_pair(far, 1)

    total = jnp.zeros((toks, feat), F32)
    for g in range(slabs):
        blocks = pl.ds(g * group, group)
        local_copy(homing.at[blocks], homing.at[blocks], home_recv.at[g]).wait()
        total = total + lax.dot_general(
            onehot[g * block : (g + 1) * block, :],
            homing[g * group : (g + 1) * group].reshape(block, feat),
            (((0,), (0,)), ((), ())),
            preferred_element_type=F32,
        )
    gin[...] = total.astype(BF16)

    half = nodes // 2
    pair_id = lax.broadcasted_iota(jnp.int32, paired.shape, 1)
    flag = jnp.sum(jnp.where(pair_id == lax.rem(me, half), paired[...].astype(F32), 0.0), axis=1, keepdims=True)

    def finish(i, carry):
        own_copy(i).wait_recv()
        value = own[i].astype(F32) + flag * other[i].astype(F32)
        gdown[pl.ds(pl.multiple_of(i * wide_own, wide_own), wide_own), :] = value.astype(BF16)
        return carry

    lax.fori_loop(0, own.shape[0], finish, 0)

    rest = rows_out.at[pl.ds(0, nodes - 1)]
    local_copy(rest, rest, rows_send).wait()
    local_copy(rest, rest, home_send).wait()
    for q in range(slabs):
        remote(part.at[q, 1 - core], mate.at[q], mate_send.at[q], mate_recv.at[q], local=mate_at).wait_send()
        for p in range(PIECES):
            held = dhid.at[q, core, piece(p)]
            remote(held, held, core_send.at[q, p], core_recv.at[q, p], local=mate_at).wait_send()
    for p in range(PIECES):
        for j in range(far):
            along("long", j, p).wait_send()
            hop("long", j, p).wait_send()
        for j in range(near):
            along("short", j, p).wait_send()
            hop("short", j, p).wait_send()
    for i in range(own.shape[0]):
        own_copy(i).wait_send()


def body(depth, grad_out, gate_prob, routes, paired, saved_pre, w_gate, w_up, w_down):
    toks, feat = grad_out.shape
    nodes, cap, hidden = saved_pre.shape[1], saved_pre.shape[2], saved_pre.shape[4]
    slabs = lax.axis_size("local") // 2
    rows = nodes * cap
    block = rows // slabs
    share = block // 2
    group = nodes // slabs
    far = slabs // 2
    near = slabs - 1 - far
    slots = max(near, 1)
    pieces_own = max(1, hidden // 128)
    vmem, dma = pltpu.VMEM, pltpu.SemaphoreType.DMA
    scratch = [
        vmem((nodes, toks), F32),
        vmem((nodes, toks), F32),
        vmem((rows, toks), BF16),
        vmem((nodes, cap, feat), BF16),
        vmem((nodes, cap, feat), BF16),
        vmem((nodes, cap, 2, hidden), BF16),
        vmem((feat, hidden), BF16),
        vmem((feat, hidden), BF16),
        vmem((hidden, feat), BF16),
        vmem((rows, hidden), F32),
        vmem((rows, hidden), F32),
        vmem((block, hidden), F32),
        vmem((slabs, hidden, block), BF16),
        vmem((slabs, 2, share, hidden), BF16),
        vmem((slabs, share, hidden), BF16),
        vmem((far, share, hidden), BF16),
        vmem((far, share, hidden), BF16),
        vmem((slots, share, hidden), BF16),
        vmem((slots, share, hidden), BF16),
        vmem((slabs, 2, share, hidden), BF16),
        vmem((nodes, cap, feat), BF16),
        vmem((nodes, cap, feat), BF16),
        vmem((pieces_own, hidden // pieces_own, feat), BF16),
        vmem((pieces_own, hidden // pieces_own, feat), BF16),
        dma((slabs,)),
        dma((3,)),
        dma,
        dma((slabs,)),
        dma((slabs,)),
        dma((slabs,)),
        dma((far, PIECES)),
        dma((far, PIECES)),
        dma((slots, PIECES)),
        dma((slots, PIECES)),
        dma((pieces_own,)),
        dma((pieces_own,)),
        dma((far, PIECES)),
        dma((far, PIECES)),
        dma((slots, PIECES)),
        dma((slots, PIECES)),
        dma((slabs, PIECES)),
        dma((slabs, PIECES)),
        dma,
        dma((slabs,)),
    ]
    whole = pl.BlockSpec(memory_space=pltpu.VMEM)
    stay = pl.BlockSpec(memory_space=pl.ANY)
    grad_in, grad_down = pl.pallas_call(
        functools.partial(kernel, depth),
        out_shape=(
            jax.ShapeDtypeStruct((toks, feat), BF16),
            jax.ShapeDtypeStruct((hidden, feat), BF16),
        ),
        in_specs=[whole] * 4 + [stay] * 4,
        out_specs=(whole, whole),
        scratch_shapes=scratch,
        compiler_params=pltpu.CompilerParams(
            collective_id=0, has_side_effects=True, vmem_limit_bytes=60 * 1024 * 1024
        ),
        name="expert_backward",
    )(grad_out, gate_prob.T, routes.T, paired[None, :], saved_pre, w_gate, w_up, w_down)
    return grad_in, grad_down[None]


def solution(mesh, depth=DEPTH):
    in_specs = (
        P("node", "local"),
        P("node", None),
        P("node", None),
        P(),
        P("node", None, None, None, None),
        P("node", "local", None),
        P("node", "local", None),
        P("node", None, "local"),
    )
    out_specs = (P("node", "local"), P("node", None, "local"))
    return jax.shard_map(
        functools.partial(body, depth), mesh=mesh, in_specs=in_specs, out_specs=out_specs, check_vma=False
    )
```

```python
import functools

import jax
import jax.numpy as jnp
from jax import lax
from jax.experimental import pallas as pl
from jax.experimental.pallas import tpu as pltpu
from jax.sharding import PartitionSpec as P

MESH = pl.DeviceIdType.MESH
DEPTH = 8
F32 = jnp.float32
BF16 = jnp.bfloat16
NT = (((1,), (1,)), ((), ()))
PIECES = 2


def remote(src, dst, send, recv, **where):
    return pltpu.make_async_remote_copy(
        src_ref=src, dst_ref=dst, send_sem=send, recv_sem=recv, device_id=where, device_id_type=MESH
    )


def local_copy(src, dst, sem):
    return pltpu.make_async_copy(src, dst, sem)


def kernel(
    depth,
    grad_out, gate, routes, paired, pre_hbm, wg_hbm, wu_hbm, wd_hbm,
    gin, gdown,
    code, gates, onehot, rows_out, rows_in, pre, wg, wu, wd, fgate, fup, act, act_t,
    part, mate, long_out, long_in, short_out, short_in, dhid, back, homing, own, rows_two, act_out, act_two,
    pre_sem, w_sem, rows_send, rows_recv, mate_send, mate_recv,
    long_send, long_recv, short_send, short_recv, two_send, two_recv, twin_send, twin_recv,
    act_up_send, act_up_recv, act_down_send, act_down_recv, act_core_send, act_core_recv,
    up_send, up_recv, down_send, down_recv, core_send, core_recv, home_send, home_recv,
):
    nodes, cap, feat = rows_out.shape
    slabs = part.shape[0]
    hidden = part.shape[3]
    share = part.shape[2]
    block = 2 * share
    group = nodes // slabs
    wide = nodes // depth
    tops, toks = routes.shape
    far, near = slabs // 2, slabs - 1 - slabs // 2
    size = share // PIECES

    me = lax.axis_index("node")
    at = lax.axis_index("local")
    my_x, my_z = me // depth, me % depth
    my_y, core = at // 2, at % 2
    sign = 1 - 2 * core
    mate_at = my_y * 2 + 1 - core
    twin = lax.rem(me + nodes // 2, nodes)

    def slab_of(step):
        return lax.rem(my_y + step + slabs, slabs)

    ahead = slab_of(sign) * 2 + core
    behind = slab_of(-sign) * 2 + core

    def offset_of(place):
        q, dz = place // depth, place % depth
        return lax.rem(q - dz + wide * depth, wide), dz

    def node_ahead(dx, dz):
        return lax.rem(my_x + dx, wide) * depth + lax.rem(my_z + dz, depth)

    def node_back(dx, dz):
        return lax.rem(my_x - dx + wide, wide) * depth + lax.rem(my_z - dz + depth, depth)

    def turn(i):
        k = far - (i + 1) // 2
        return lax.rem(my_y + jnp.where(i % 2 == 0, -k, k) + slabs, slabs)

    barrier = pltpu.get_barrier_semaphore()

    def greet(k, carry):
        pl.semaphore_signal(barrier, inc=1, device_id={"node": lax.rem(me + k, nodes)}, device_id_type=MESH)
        return carry

    lax.fori_loop(1, nodes, greet, 0)
    for other_at in (mate_at, ahead, behind):
        pl.semaphore_signal(barrier, inc=1, device_id={"local": other_at}, device_id_type=MESH)

    loads = [local_copy(a.at[0], b, w_sem.at[i]) for i, (a, b) in enumerate(((wd_hbm, wd), (wg_hbm, wg), (wu_hbm, wu)))]

    def load_pre(n, carry):
        place = lax.rem(n + my_y * group, nodes)
        dx, dz = offset_of(place)
        local_copy(pre_hbm.at[0, node_ahead(dx, dz)], pre.at[place], pre_sem.at[place // group]).start()
        return carry

    lax.fori_loop(0, nodes, load_pre, 0)
    for load in loads:
        load.start()

    slot_id = lax.broadcasted_iota(jnp.int32, (nodes, toks), 0)
    named = jnp.zeros((nodes, toks), F32)
    gate_of = jnp.zeros((nodes, toks), F32)
    for k in range(tops):
        hit = routes[k : k + 1, :] == slot_id
        named = jnp.where(hit, 1.0, named)
        gate_of = jnp.where(hit, gate[k : k + 1, :], gate_of)
    earlier = lax.broadcasted_iota(jnp.int32, (toks, toks), 0) < lax.broadcasted_iota(jnp.int32, (toks, toks), 1)
    rank = jnp.dot(named.astype(BF16), jnp.where(earlier, 1.0, 0.0).astype(BF16), preferred_element_type=F32)
    code[...] = jnp.where(named > 0.0, rank, -1.0)
    gates[...] = gate_of
    some = min(8, nodes)

    def fill(i, carry):
        slots = pl.ds(pl.multiple_of(i * some, some), some)
        want = lax.broadcasted_iota(jnp.int32, (some, cap, toks), 1).astype(F32)
        hit = code[slots, :][:, None, :] == want
        scale = jnp.sum(jnp.where(hit, gates[slots, :][:, None, :], 0.0), axis=2, keepdims=True)
        picks = jnp.where(hit, 1.0, 0.0).reshape(some * cap, toks).astype(BF16)
        onehot[pl.ds(pl.multiple_of(i * some * cap, some * cap), some * cap), :] = picks
        values = jnp.dot(picks, grad_out[...], preferred_element_type=F32)
        values = values.reshape(some, cap, feat) * scale
        rows_out[slots] = values.astype(BF16)
        return carry

    lax.fori_loop(0, nodes // some, fill, 0)

    def factors(n, carry):
        q = lax.rem(my_y + n, slabs)
        blocks = pl.ds(pl.multiple_of(q * group, group), group)
        local_copy(pre.at[blocks], pre.at[blocks], pre_sem.at[q]).wait()

        def one(i, carry):
            place = q * group + i
            both = pre[place].astype(F32)
            gval, uval = both[:, 0, :], both[:, 1, :]
            sigm = jax.nn.sigmoid(gval)
            silu = gval * sigm
            these = pl.ds(pl.multiple_of(place * cap, cap), cap)
            fgate[these, :] = uval * sigm * (1.0 + gval * (1.0 - sigm))
            fup[these, :] = silu
            act[pl.ds(pl.multiple_of(i * cap, cap), cap), :] = silu * uval
            return carry

        lax.fori_loop(0, group, one, 0)
        act_t[q] = act[...].T.astype(BF16)
        return carry

    factors(0, 0)
    act_out[...] = act[pl.ds(pl.multiple_of(core * share, share), share), :].astype(BF16)

    pl.semaphore_wait(barrier, nodes - 1 + 3)

    def send_rows(n, carry):
        i, dz = n // depth, n % depth
        q = turn(i)
        dx = lax.rem(q - dz + wide * depth, wide)
        target = node_back(dx, dz)
        place = q * depth + dz

        @pl.when(target != me)
        def _():
            remote(rows_out.at[target], rows_in.at[place], rows_send, rows_recv.at[q], node=target).start()

        @pl.when(target == me)
        def _():
            local_copy(rows_out.at[target], rows_in.at[place], rows_recv.at[q]).start()

        return carry

    def send_twin(n, carry):
        i, dz = n // depth, n % depth
        q = turn(i)
        dx = lax.rem(q - dz + wide * depth, wide)
        slot = node_back(dx, dz)
        target = lax.rem(slot + nodes // 2, nodes)
        place = q * depth + dz

        @pl.when(target != me)
        def _():
            remote(rows_out.at[slot], rows_two.at[place], two_send, two_recv, node=target).start()

        @pl.when(target == me)
        def _():
            local_copy(rows_out.at[slot], rows_two.at[place], two_recv).start()

        return carry

    def to_twin():
        return remote(act_out, act_two.at[my_y, core], twin_send, twin_recv, node=twin)

    first = min(slabs, 3) * group
    lax.fori_loop(0, first, send_rows, 0)
    to_twin().start()
    lax.fori_loop(first, nodes, send_rows, 0)

    lax.fori_loop(1, slabs, factors, 0)
    loads[0].wait()

    def product(i, carry):
        q = turn(i)
        blocks = pl.ds(pl.multiple_of(q * group, group), group)
        local_copy(rows_in.at[blocks], rows_in.at[blocks], rows_recv.at[q]).wait()
        value = lax.dot_general(rows_in[blocks].reshape(block, feat), wd[...], NT, preferred_element_type=F32)
        part[q] = value.astype(BF16).reshape(2, share, hidden)
        remote(part.at[q, 1 - core], mate.at[q], mate_send.at[q], mate_recv.at[q], local=mate_at).start()
        return carry

    def piece(p):
        return pl.ds(p * size, size)

    def mine(q, p):
        return part[q, core, piece(p), :].astype(F32) + mate[q, piece(p), :].astype(F32)

    def wait_mate(q):
        remote(part.at[q, 1 - core], mate.at[q], mate_send.at[q], mate_recv.at[q], local=mate_at).wait_recv()

    def along(kind, j, p):
        if kind == "long":
            return remote(
                long_out.at[j, piece(p)], long_in.at[j, piece(p)], long_send.at[j, p], long_recv.at[j, p], local=ahead
            )
        return remote(
            short_out.at[j, piece(p)], short_in.at[j, piece(p)], short_send.at[j, p], short_recv.at[j, p], local=behind
        )

    waited = set()

    def reduce_step(j):
        chains = [("long", far - j)] + ([("short", -(near - j))] if j < near else [])
        for _, step in chains:
            if step not in waited:
                wait_mate(slab_of(step * sign))
                waited.add(step)
        for p in range(PIECES):
            for kind, step in chains:
                total = mine(slab_of(step * sign), p)
                if j > 0:
                    along(kind, j - 1, p).wait_recv()
                    total = total + (long_in if kind == "long" else short_in)[j - 1, piece(p), :].astype(F32)
                (long_out if kind == "long" else short_out)[j, piece(p), :] = total.astype(BF16)
                along(kind, j, p).start()

    def hop(array, kind, k, p):
        q = slab_of(-k * sign if kind == "long" else k * sign)
        held = array.at[q, core, piece(p)]
        up, up_in, down, down_in = (
            (up_send, up_recv, down_send, down_recv)
            if array is dhid
            else (act_up_send, act_up_recv, act_down_send, act_down_recv)
        )
        if kind == "long":
            return remote(held, held, up.at[k, p], up_in.at[k, p], local=ahead)
        return remote(held, held, down.at[k, p], down_in.at[k, p], local=behind)

    def cross(array, q, side, p):
        held = array.at[q, side, piece(p)]
        out, into = (core_send, core_recv) if array is dhid else (act_core_send, act_core_recv)
        return remote(held, held, out.at[q, p], into.at[q, p], local=mate_at)

    def spread(array, k):
        for p in range(PIECES):
            if k > 0:
                hop(array, "long", k - 1, p).wait_recv()
            if k < far:
                hop(array, "long", k, p).start()
            cross(array, slab_of(-k * sign), core, p).start()
            if 0 < k <= near:
                hop(array, "short", k - 1, p).wait_recv()
            if k < near:
                hop(array, "short", k, p).start()
            if 0 < k <= near:
                cross(array, slab_of(k * sign), core, p).start()

    wide_own = own.shape[1]
    count = own.shape[0]

    def gradient(i, rows):
        these = pl.ds(pl.multiple_of(i * wide_own, wide_own), wide_own)
        value = jnp.zeros((wide_own, feat), F32)
        for q in range(slabs):
            value = value + jnp.dot(
                act_t[q, these, :], rows[q * group : (q + 1) * group].reshape(block, feat), preferred_element_type=F32
            )
        return value.astype(BF16)

    def own_piece(i, carry):
        own[i] = gradient(i, rows_in)
        return carry

    lax.fori_loop(0, min(slabs, 3), product, 0)
    reduce_step(0)
    lax.fori_loop(min(slabs, 3), min(slabs, 5), product, 0)
    if far > 1:
        reduce_step(1)
    lax.fori_loop(0, nodes, send_twin, 0)
    to_twin().wait_recv()
    spread(act_two, 0)
    lax.fori_loop(min(slabs, 5), slabs, product, 0)
    if far > 2:
        reduce_step(2)
    lax.fori_loop(0, count // 2, own_piece, 0)
    spread(act_two, 1)
    for j in range(3, far):
        reduce_step(j)
    lax.fori_loop(count // 2, count, own_piece, 0)
    if far > 1:
        spread(act_two, 2)

    wait_mate(my_y)
    for p in range(PIECES):
        total = mine(my_y, p)
        along("long", far - 1, p).wait_recv()
        total = total + long_in[far - 1, piece(p), :].astype(F32)
        if near > 0:
            along("short", near - 1, p).wait_recv()
            total = total + short_in[near - 1, piece(p), :].astype(F32)
        dhid[my_y, core, piece(p), :] = total.astype(BF16)

    spread(dhid, 0)
    loads[1].wait()
    loads[2].wait()

    def send_back(n, q):
        place = q * depth + lax.rem(n + my_z, depth)
        dx, dz = offset_of(place)
        target = node_ahead(dx, dz)

        @pl.when(target != me)
        def _():
            remote(back.at[place], homing.at[me], home_send, home_recv.at[me // group], node=target).start()

        @pl.when(target == me)
        def _():
            local_copy(back.at[place], homing.at[me], home_recv.at[me // group]).start()

        return q

    def rows_back(q):
        for p in range(PIECES):
            cross(dhid, q, 1 - core, p).wait_recv()
        these = pl.ds(pl.multiple_of(q * block, block), block)
        value = dhid[q].reshape(block, hidden).astype(F32)
        dgate = (value * fgate[these, :]).astype(BF16)
        dup = (value * fup[these, :]).astype(BF16)
        result = lax.dot_general(dgate, wg[...], NT, preferred_element_type=F32)
        result = result + lax.dot_general(dup, wu[...], NT, preferred_element_type=F32)
        back[pl.ds(pl.multiple_of(q * group, group), group)] = result.astype(BF16).reshape(group, cap, feat)
        lax.fori_loop(0, group, send_back, q)

    def rows_back_pair(k, count):
        def body(i, carry):
            rows_back(slab_of(jnp.where(i == 0, -k, k)))
            return carry

        lax.fori_loop(0, count, body, 0)

    for k in range(1, far + 1):
        spread(dhid, k)
        rows_back_pair(k - 1, 1 if k == 1 else 2)
        if 2 < k + 2 <= far:
            spread(act_two, k + 2)
    rows_back_pair(far, 1)

    half = nodes // 2
    pair_id = lax.broadcasted_iota(jnp.int32, paired.shape, 1)
    flag = jnp.sum(jnp.where(pair_id == lax.rem(me, half), paired[...].astype(F32), 0.0), axis=1, keepdims=True)

    def turned(q, carry):
        for p in range(PIECES):
            cross(act_two, q, 1 - core, p).wait_recv()
        act_t[q] = act_two[q].reshape(block, hidden).astype(F32).T.astype(BF16)
        return carry

    lax.fori_loop(0, slabs, turned, 0)
    local_copy(rows_two, rows_two, two_recv).wait()

    def finish(i, carry):
        value = own[i].astype(F32) + flag * gradient(i, rows_two).astype(F32)
        gdown[pl.ds(pl.multiple_of(i * wide_own, wide_own), wide_own), :] = value.astype(BF16)
        return carry

    lax.fori_loop(0, count, finish, 0)

    total = jnp.zeros((toks, feat), F32)
    for g in range(slabs):
        blocks = pl.ds(g * group, group)
        local_copy(homing.at[blocks], homing.at[blocks], home_recv.at[g]).wait()
        total = total + lax.dot_general(
            onehot[g * block : (g + 1) * block, :],
            homing[g * group : (g + 1) * group].reshape(block, feat),
            (((0,), (0,)), ((), ())),
            preferred_element_type=F32,
        )
    gin[...] = total.astype(BF16)

    rest = rows_out.at[pl.ds(0, nodes - 1)]
    local_copy(rest, rest, rows_send).wait()
    local_copy(rest, rest, home_send).wait()
    local_copy(rest, rest, two_send).wait()
    to_twin().wait_send()
    for q in range(slabs):
        remote(part.at[q, 1 - core], mate.at[q], mate_send.at[q], mate_recv.at[q], local=mate_at).wait_send()
        for p in range(PIECES):
            for array in (dhid, act_two):
                cross(array, q, core, p).wait_send()
    for p in range(PIECES):
        for j in range(far):
            along("long", j, p).wait_send()
            for array in (dhid, act_two):
                hop(array, "long", j, p).wait_send()
        for j in range(near):
            along("short", j, p).wait_send()
            for array in (dhid, act_two):
                hop(array, "short", j, p).wait_send()


def body(depth, grad_out, gate_prob, routes, paired, saved_pre, w_gate, w_up, w_down):
    toks, feat = grad_out.shape
    nodes, cap, hidden = saved_pre.shape[1], saved_pre.shape[2], saved_pre.shape[4]
    slabs = lax.axis_size("local") // 2
    rows = nodes * cap
    block = rows // slabs
    share = block // 2
    group = nodes // slabs
    far = slabs // 2
    near = slabs - 1 - far
    slots = max(near, 1)
    pieces_own = max(1, hidden // 128)
    vmem, dma = pltpu.VMEM, pltpu.SemaphoreType.DMA
    scratch = [
        vmem((nodes, toks), F32),
        vmem((nodes, toks), F32),
        vmem((rows, toks), BF16),
        vmem((nodes, cap, feat), BF16),
        vmem((nodes, cap, feat), BF16),
        vmem((nodes, cap, 2, hidden), BF16),
        vmem((feat, hidden), BF16),
        vmem((feat, hidden), BF16),
        vmem((hidden, feat), BF16),
        vmem((rows, hidden), F32),
        vmem((rows, hidden), F32),
        vmem((block, hidden), F32),
        vmem((slabs, hidden, block), BF16),
        vmem((slabs, 2, share, hidden), BF16),
        vmem((slabs, share, hidden), BF16),
        vmem((far, share, hidden), BF16),
        vmem((far, share, hidden), BF16),
        vmem((slots, share, hidden), BF16),
        vmem((slots, share, hidden), BF16),
        vmem((slabs, 2, share, hidden), BF16),
        vmem((nodes, cap, feat), BF16),
        vmem((nodes, cap, feat), BF16),
        vmem((pieces_own, hidden // pieces_own, feat), BF16),
        vmem((nodes, cap, feat), BF16),
        vmem((share, hidden), BF16),
        vmem((slabs, 2, share, hidden), BF16),
        dma((slabs,)),
        dma((3,)),
        dma,
        dma((slabs,)),
        dma((slabs,)),
        dma((slabs,)),
        dma((far, PIECES)),
        dma((far, PIECES)),
        dma((slots, PIECES)),
        dma((slots, PIECES)),
        dma,
        dma,
        dma,
        dma,
        dma((far, PIECES)),
        dma((far, PIECES)),
        dma((slots, PIECES)),
        dma((slots, PIECES)),
        dma((slabs, PIECES)),
        dma((slabs, PIECES)),
        dma((far, PIECES)),
        dma((far, PIECES)),
        dma((slots, PIECES)),
        dma((slots, PIECES)),
        dma((slabs, PIECES)),
        dma((slabs, PIECES)),
        dma,
        dma((slabs,)),
    ]
    whole = pl.BlockSpec(memory_space=pltpu.VMEM)
    stay = pl.BlockSpec(memory_space=pl.ANY)
    grad_in, grad_down = pl.pallas_call(
        functools.partial(kernel, depth),
        out_shape=(
            pltpu.VMEM((toks, feat), BF16),
            pltpu.VMEM((hidden, feat), BF16),
        ),
        in_specs=[whole] * 4 + [stay] * 4,
        out_specs=(whole, whole),
        scratch_shapes=scratch,
        compiler_params=pltpu.CompilerParams(
            collective_id=0, has_side_effects=True, vmem_limit_bytes=60 * 1024 * 1024
        ),
        name="expert_backward",
    )(grad_out, gate_prob.T, routes.T, paired[None, :], saved_pre, w_gate, w_up, w_down)
    return grad_in, grad_down[None]


def solution(mesh, depth=DEPTH):
    in_specs = (
        P("node", "local"),
        P("node", None),
        P("node", None),
        P(),
        P("node", None, None, None, None),
        P("node", "local", None),
        P("node", "local", None),
        P("node", None, "local"),
    )
    out_specs = (P("node", "local"), P("node", None, "local"))
    return jax.shard_map(
        functools.partial(body, depth), mesh=mesh, in_specs=in_specs, out_specs=out_specs, check_vma=False
    )
```

```python
import functools

import jax
import jax.numpy as jnp
from jax import lax
from jax.experimental import pallas as pl
from jax.experimental.pallas import tpu as pltpu
from jax.sharding import PartitionSpec as P

MESH = pl.DeviceIdType.MESH
DEPTH = 8
F32 = jnp.float32
BF16 = jnp.bfloat16
NT = (((1,), (1,)), ((), ()))
PIECES = 4


def remote(src, dst, send, recv, **where):
    return pltpu.make_async_remote_copy(
        src_ref=src, dst_ref=dst, send_sem=send, recv_sem=recv, device_id=where, device_id_type=MESH
    )


def local_copy(src, dst, sem):
    return pltpu.make_async_copy(src, dst, sem)


def kernel(
    depth,
    grad_out, gate, routes, paired, pre_hbm, wg_hbm, wu_hbm, wd_hbm,
    gin, gdown,
    code, gates, onehot, rows_out, rows_in, pre, wg, wu, wd, fgate, fup, act, act_t,
    part, mate, long_out, long_in, short_out, short_in, dhid, back, homing, own, rows_two, act_out, act_two,
    pre_sem, w_sem, rows_send, rows_recv, mate_send, mate_recv,
    long_send, long_recv, short_send, short_recv, two_send, two_recv, twin_send, twin_recv,
    act_up_send, act_up_recv, act_down_send, act_down_recv, act_core_send, act_core_recv,
    up_send, up_recv, down_send, down_recv, core_send, core_recv, home_send, home_recv,
):
    nodes, cap, feat = rows_out.shape
    slabs = part.shape[0]
    hidden = part.shape[3]
    share = part.shape[2]
    block = 2 * share
    group = nodes // slabs
    wide = nodes // depth
    tops, toks = routes.shape
    far, near = slabs // 2, slabs - 1 - slabs // 2
    size = share // PIECES

    me = lax.axis_index("node")
    at = lax.axis_index("local")
    my_x, my_z = me // depth, me % depth
    my_y, core = at // 2, at % 2
    sign = 1 - 2 * core
    mate_at = my_y * 2 + 1 - core
    twin = lax.rem(me + nodes // 2, nodes)

    def slab_of(step):
        return lax.rem(my_y + step + slabs, slabs)

    ahead = slab_of(sign) * 2 + core
    behind = slab_of(-sign) * 2 + core

    def offset_of(place):
        q, dz = place // depth, place % depth
        return lax.rem(q - dz + wide * depth, wide), dz

    def node_ahead(dx, dz):
        return lax.rem(my_x + dx, wide) * depth + lax.rem(my_z + dz, depth)

    def node_back(dx, dz):
        return lax.rem(my_x - dx + wide, wide) * depth + lax.rem(my_z - dz + depth, depth)

    def turn(i):
        k = far - (i + 1) // 2
        return lax.rem(my_y + jnp.where(i % 2 == 0, -k, k) + slabs, slabs)

    barrier = pltpu.get_barrier_semaphore()

    def greet(k, carry):
        pl.semaphore_signal(barrier, inc=1, device_id={"node": lax.rem(me + k, nodes)}, device_id_type=MESH)
        return carry

    lax.fori_loop(1, nodes, greet, 0)
    for other_at in (mate_at, ahead, behind):
        pl.semaphore_signal(barrier, inc=1, device_id={"local": other_at}, device_id_type=MESH)

    loads = [local_copy(a.at[0], b, w_sem.at[i]) for i, (a, b) in enumerate(((wd_hbm, wd), (wg_hbm, wg), (wu_hbm, wu)))]

    def load_pre(n, carry):
        place = lax.rem(n + my_y * group, nodes)
        dx, dz = offset_of(place)
        local_copy(pre_hbm.at[0, node_ahead(dx, dz)], pre.at[place], pre_sem.at[place // group]).start()
        return carry

    lax.fori_loop(0, nodes, load_pre, 0)
    for load in loads:
        load.start()

    slot_id = lax.broadcasted_iota(jnp.int32, (nodes, toks), 0)
    named = jnp.zeros((nodes, toks), F32)
    gate_of = jnp.zeros((nodes, toks), F32)
    for k in range(tops):
        hit = routes[k : k + 1, :] == slot_id
        named = jnp.where(hit, 1.0, named)
        gate_of = jnp.where(hit, gate[k : k + 1, :], gate_of)
    earlier = lax.broadcasted_iota(jnp.int32, (toks, toks), 0) < lax.broadcasted_iota(jnp.int32, (toks, toks), 1)
    rank = jnp.dot(named.astype(BF16), jnp.where(earlier, 1.0, 0.0).astype(BF16), preferred_element_type=F32)
    code[...] = jnp.where(named > 0.0, rank, -1.0)
    gates[...] = gate_of
    some = min(8, nodes)

    def fill(i, carry):
        slots = pl.ds(pl.multiple_of(i * some, some), some)
        want = lax.broadcasted_iota(jnp.int32, (some, cap, toks), 1).astype(F32)
        hit = code[slots, :][:, None, :] == want
        scale = jnp.sum(jnp.where(hit, gates[slots, :][:, None, :], 0.0), axis=2, keepdims=True)
        picks = jnp.where(hit, 1.0, 0.0).reshape(some * cap, toks).astype(BF16)
        onehot[pl.ds(pl.multiple_of(i * some * cap, some * cap), some * cap), :] = picks
        values = jnp.dot(picks, grad_out[...], preferred_element_type=F32)
        values = values.reshape(some, cap, feat) * scale
        rows_out[slots] = values.astype(BF16)
        return carry

    lax.fori_loop(0, nodes // some, fill, 0)

    def factors(n, carry):
        q = lax.rem(my_y + n, slabs)
        blocks = pl.ds(pl.multiple_of(q * group, group), group)
        local_copy(pre.at[blocks], pre.at[blocks], pre_sem.at[q]).wait()

        def one(i, carry):
            place = q * group + i
            both = pre[place].astype(F32)
            gval, uval = both[:, 0, :], both[:, 1, :]
            sigm = jax.nn.sigmoid(gval)
            silu = gval * sigm
            these = pl.ds(pl.multiple_of(place * cap, cap), cap)
            fgate[these, :] = uval * sigm * (1.0 + gval * (1.0 - sigm))
            fup[these, :] = silu
            act[pl.ds(pl.multiple_of(i * cap, cap), cap), :] = silu * uval
            return carry

        lax.fori_loop(0, group, one, 0)
        act_t[q] = act[...].T.astype(BF16)
        return carry

    pl.semaphore_wait(barrier, nodes - 1 + 3)

    def send_rows(n, carry):
        i, dz = n // depth, n % depth
        q = turn(i)
        dx = lax.rem(q - dz + wide * depth, wide)
        target = node_back(dx, dz)
        place = q * depth + dz

        @pl.when(target != me)
        def _():
            remote(rows_out.at[target], rows_in.at[place], rows_send, rows_recv.at[q], node=target).start()

        @pl.when(target == me)
        def _():
            local_copy(rows_out.at[target], rows_in.at[place], rows_recv.at[q]).start()

        return carry

    def send_twin(n, carry):
        i, dz = n // depth, n % depth
        q = turn(i)
        dx = lax.rem(q - dz + wide * depth, wide)
        slot = node_back(dx, dz)
        target = lax.rem(slot + nodes // 2, nodes)
        place = q * depth + dz

        @pl.when(target != me)
        def _():
            remote(rows_out.at[slot], rows_two.at[place], two_send, two_recv, node=target).start()

        @pl.when(target == me)
        def _():
            local_copy(rows_out.at[slot], rows_two.at[place], two_recv).start()

        return carry

    def to_twin():
        return remote(act_out, act_two.at[my_y, core], twin_send, twin_recv, node=twin)

    lax.fori_loop(0, nodes, send_rows, 0)
    factors(0, 0)
    act_out[...] = act[pl.ds(pl.multiple_of(core * share, share), share), :].astype(BF16)

    lax.fori_loop(1, slabs, factors, 0)
    loads[0].wait()

    def product(i, carry):
        q = turn(i)
        blocks = pl.ds(pl.multiple_of(q * group, group), group)
        local_copy(rows_in.at[blocks], rows_in.at[blocks], rows_recv.at[q]).wait()
        value = lax.dot_general(rows_in[blocks].reshape(block, feat), wd[...], NT, preferred_element_type=F32)
        part[q] = value.astype(BF16).reshape(2, share, hidden)
        remote(part.at[q, 1 - core], mate.at[q], mate_send.at[q], mate_recv.at[q], local=mate_at).start()
        return carry

    def piece(p):
        return pl.ds(p * size, size)

    def mine(q, p):
        return part[q, core, piece(p), :].astype(F32) + mate[q, piece(p), :].astype(F32)

    def wait_mate(q):
        remote(part.at[q, 1 - core], mate.at[q], mate_send.at[q], mate_recv.at[q], local=mate_at).wait_recv()

    def along(kind, j, p):
        if kind == "long":
            return remote(
                long_out.at[j, piece(p)], long_in.at[j, piece(p)], long_send.at[j, p], long_recv.at[j, p], local=ahead
            )
        return remote(
            short_out.at[j, piece(p)], short_in.at[j, piece(p)], short_send.at[j, p], short_recv.at[j, p], local=behind
        )

    waited = set()

    def reduce_step(j):
        chains = [("long", far - j)] + ([("short", -(near - j))] if j < near else [])
        for _, step in chains:
            if step not in waited:
                wait_mate(slab_of(step * sign))
                waited.add(step)
        for p in range(PIECES):
            for kind, step in chains:
                total = mine(slab_of(step * sign), p)
                if j > 0:
                    along(kind, j - 1, p).wait_recv()
                    total = total + (long_in if kind == "long" else short_in)[j - 1, piece(p), :].astype(F32)
                (long_out if kind == "long" else short_out)[j, piece(p), :] = total.astype(BF16)
                along(kind, j, p).start()

    def hop(array, kind, k, p):
        q = slab_of(-k * sign if kind == "long" else k * sign)
        held = array.at[q, core, piece(p)]
        up, up_in, down, down_in = (
            (up_send, up_recv, down_send, down_recv)
            if array is dhid
            else (act_up_send, act_up_recv, act_down_send, act_down_recv)
        )
        if kind == "long":
            return remote(held, held, up.at[k, p], up_in.at[k, p], local=ahead)
        return remote(held, held, down.at[k, p], down_in.at[k, p], local=behind)

    def cross(array, q, side, p):
        held = array.at[q, side, piece(p)]
        out, into = (core_send, core_recv) if array is dhid else (act_core_send, act_core_recv)
        return remote(held, held, out.at[q, p], into.at[q, p], local=mate_at)

    def spread(array, k):
        for p in range(PIECES):
            if k > 0:
                hop(array, "long", k - 1, p).wait_recv()
            if k < far:
                hop(array, "long", k, p).start()
            cross(array, slab_of(-k * sign), core, p).start()
            if 0 < k <= near:
                hop(array, "short", k - 1, p).wait_recv()
            if k < near:
                hop(array, "short", k, p).start()
            if 0 < k <= near:
                cross(array, slab_of(k * sign), core, p).start()

    wide_own = own.shape[1]
    count = own.shape[0]

    def gradient(i, rows):
        these = pl.ds(pl.multiple_of(i * wide_own, wide_own), wide_own)
        value = jnp.zeros((wide_own, feat), F32)
        for q in range(slabs):
            value = value + jnp.dot(
                act_t[q, these, :], rows[q * group : (q + 1) * group].reshape(block, feat), preferred_element_type=F32
            )
        return value.astype(BF16)

    def own_piece(i, carry):
        own[i] = gradient(i, rows_in)
        return carry

    lax.fori_loop(0, min(slabs, 3), product, 0)
    reduce_step(0)
    lax.fori_loop(min(slabs, 3), min(slabs, 5), product, 0)
    if far > 1:
        reduce_step(1)
    to_twin().start()
    lax.fori_loop(0, nodes, send_twin, 0)
    lax.fori_loop(min(slabs, 5), slabs, product, 0)
    if far > 2:
        reduce_step(2)
    lax.fori_loop(0, count // 2, own_piece, 0)
    for j in range(3, far):
        reduce_step(j)
    lax.fori_loop(count // 2, count, own_piece, 0)

    wait_mate(my_y)
    for p in range(PIECES):
        total = mine(my_y, p)
        along("long", far - 1, p).wait_recv()
        total = total + long_in[far - 1, piece(p), :].astype(F32)
        if near > 0:
            along("short", near - 1, p).wait_recv()
            total = total + short_in[near - 1, piece(p), :].astype(F32)
        dhid[my_y, core, piece(p), :] = total.astype(BF16)

    spread(dhid, 0)
    loads[1].wait()
    loads[2].wait()

    def send_back(n, q):
        place = q * depth + lax.rem(n + my_z, depth)
        dx, dz = offset_of(place)
        target = node_ahead(dx, dz)

        @pl.when(target != me)
        def _():
            remote(back.at[place], homing.at[me], home_send, home_recv.at[me // group], node=target).start()

        @pl.when(target == me)
        def _():
            local_copy(back.at[place], homing.at[me], home_recv.at[me // group]).start()

        return q

    def rows_back(q):
        for p in range(PIECES):
            cross(dhid, q, 1 - core, p).wait_recv()
        these = pl.ds(pl.multiple_of(q * block, block), block)
        value = dhid[q].reshape(block, hidden).astype(F32)
        dgate = (value * fgate[these, :]).astype(BF16)
        dup = (value * fup[these, :]).astype(BF16)
        result = lax.dot_general(dgate, wg[...], NT, preferred_element_type=F32)
        result = result + lax.dot_general(dup, wu[...], NT, preferred_element_type=F32)
        back[pl.ds(pl.multiple_of(q * group, group), group)] = result.astype(BF16).reshape(group, cap, feat)
        lax.fori_loop(0, group, send_back, q)

    def rows_back_pair(k, count):
        def body(i, carry):
            rows_back(slab_of(jnp.where(i == 0, -k, k)))
            return carry

        lax.fori_loop(0, count, body, 0)

    later = 0
    for k in range(1, far + 1):
        spread(dhid, k)
        if k >= far - 1:
            if later == 0:
                to_twin().wait_recv()
            spread(act_two, later)
            later += 1
        rows_back_pair(k - 1, 1 if k == 1 else 2)
    if later <= far:
        spread(act_two, later)
        later += 1
    rows_back_pair(far, 1)
    for k in range(later, far + 1):
        spread(act_two, k)

    half = nodes // 2
    pair_id = lax.broadcasted_iota(jnp.int32, paired.shape, 1)
    flag = jnp.sum(jnp.where(pair_id == lax.rem(me, half), paired[...].astype(F32), 0.0), axis=1, keepdims=True)

    def turned(q, carry):
        for p in range(PIECES):
            cross(act_two, q, 1 - core, p).wait_recv()
        act_t[q] = act_two[q].reshape(block, hidden).astype(F32).T.astype(BF16)
        return carry

    lax.fori_loop(0, slabs, turned, 0)
    local_copy(rows_two, rows_two, two_recv).wait()

    def finish(i, carry):
        value = own[i].astype(F32) + flag * gradient(i, rows_two).astype(F32)
        gdown[pl.ds(pl.multiple_of(i * wide_own, wide_own), wide_own), :] = value.astype(BF16)
        return carry

    lax.fori_loop(0, count, finish, 0)

    total = jnp.zeros((toks, feat), F32)
    for g in range(slabs):
        blocks = pl.ds(g * group, group)
        local_copy(homing.at[blocks], homing.at[blocks], home_recv.at[g]).wait()
        total = total + lax.dot_general(
            onehot[g * block : (g + 1) * block, :],
            homing[g * group : (g + 1) * group].reshape(block, feat),
            (((0,), (0,)), ((), ())),
            preferred_element_type=F32,
        )
    gin[...] = total.astype(BF16)

    rest = rows_out.at[pl.ds(0, nodes - 1)]
    local_copy(rest, rest, rows_send).wait()
    local_copy(rest, rest, home_send).wait()
    local_copy(rest, rest, two_send).wait()
    to_twin().wait_send()
    for q in range(slabs):
        remote(part.at[q, 1 - core], mate.at[q], mate_send.at[q], mate_recv.at[q], local=mate_at).wait_send()
        for p in range(PIECES):
            for array in (dhid, act_two):
                cross(array, q, core, p).wait_send()
    for p in range(PIECES):
        for j in range(far):
            along("long", j, p).wait_send()
            for array in (dhid, act_two):
                hop(array, "long", j, p).wait_send()
        for j in range(near):
            along("short", j, p).wait_send()
            for array in (dhid, act_two):
                hop(array, "short", j, p).wait_send()


def body(depth, grad_out, gate_prob, routes, paired, saved_pre, w_gate, w_up, w_down):
    toks, feat = grad_out.shape
    nodes, cap, hidden = saved_pre.shape[1], saved_pre.shape[2], saved_pre.shape[4]
    slabs = lax.axis_size("local") // 2
    rows = nodes * cap
    block = rows // slabs
    share = block // 2
    group = nodes // slabs
    far = slabs // 2
    near = slabs - 1 - far
    slots = max(near, 1)
    pieces_own = max(1, hidden // 128)
    vmem, dma = pltpu.VMEM, pltpu.SemaphoreType.DMA
    scratch = [
        vmem((nodes, toks), F32),
        vmem((nodes, toks), F32),
        vmem((rows, toks), BF16),
        vmem((nodes, cap, feat), BF16),
        vmem((nodes, cap, feat), BF16),
        vmem((nodes, cap, 2, hidden), BF16),
        vmem((feat, hidden), BF16),
        vmem((feat, hidden), BF16),
        vmem((hidden, feat), BF16),
        vmem((rows, hidden), F32),
        vmem((rows, hidden), F32),
        vmem((block, hidden), F32),
        vmem((slabs, hidden, block), BF16),
        vmem((slabs, 2, share, hidden), BF16),
        vmem((slabs, share, hidden), BF16),
        vmem((far, share, hidden), BF16),
        vmem((far, share, hidden), BF16),
        vmem((slots, share, hidden), BF16),
        vmem((slots, share, hidden), BF16),
        vmem((slabs, 2, share, hidden), BF16),
        vmem((nodes, cap, feat), BF16),
        vmem((nodes, cap, feat), BF16),
        vmem((pieces_own, hidden // pieces_own, feat), BF16),
        vmem((nodes, cap, feat), BF16),
        vmem((share, hidden), BF16),
        vmem((slabs, 2, share, hidden), BF16),
        dma((slabs,)),
        dma((3,)),
        dma,
        dma((slabs,)),
        dma((slabs,)),
        dma((slabs,)),
        dma((far, PIECES)),
        dma((far, PIECES)),
        dma((slots, PIECES)),
        dma((slots, PIECES)),
        dma,
        dma,
        dma,
        dma,
        dma((far, PIECES)),
        dma((far, PIECES)),
        dma((slots, PIECES)),
        dma((slots, PIECES)),
        dma((slabs, PIECES)),
        dma((slabs, PIECES)),
        dma((far, PIECES)),
        dma((far, PIECES)),
        dma((slots, PIECES)),
        dma((slots, PIECES)),
        dma((slabs, PIECES)),
        dma((slabs, PIECES)),
        dma,
        dma((slabs,)),
    ]
    whole = pl.BlockSpec(memory_space=pltpu.VMEM)
    stay = pl.BlockSpec(memory_space=pl.ANY)
    grad_in, grad_down = pl.pallas_call(
        functools.partial(kernel, depth),
        out_shape=(
            pltpu.VMEM((toks, feat), BF16),
            pltpu.VMEM((hidden, feat), BF16),
        ),
        in_specs=[whole] * 4 + [stay] * 4,
        out_specs=(whole, whole),
        scratch_shapes=scratch,
        compiler_params=pltpu.CompilerParams(
            collective_id=0, has_side_effects=True, vmem_limit_bytes=60 * 1024 * 1024
        ),
        name="expert_backward",
    )(grad_out, gate_prob.T, routes.T, paired[None, :], saved_pre, w_gate, w_up, w_down)
    return grad_in, grad_down[None]


def solution(mesh, depth=DEPTH):
    in_specs = (
        P("node", "local"),
        P("node", None),
        P("node", None),
        P(),
        P("node", None, None, None, None),
        P("node", "local", None),
        P("node", "local", None),
        P("node", None, "local"),
    )
    out_specs = (P("node", "local"), P("node", None, "local"))
    return jax.shard_map(
        functools.partial(body, depth), mesh=mesh, in_specs=in_specs, out_specs=out_specs, check_vma=False
    )
```
